128 devices in a mesh: row: 16 (over y_hi, x, core), col: 8 (over z, y_lo).
Axes of the slice: x: 4, y: 4 (y_hi: 2, y_lo: 2; y = y_hi * 2 + y_lo), z: 4, core: 2. Of those that a mesh axis runs over, the one named last changes fastest.
Arguments:
- activations: bfloat16 [4, 1024, 8192], P(None, 'col', 'row'), may hold values from -6 to 6
- member_weights: bfloat16 [4, 8192, 1024], P(None, ('col', 'row')), may hold values from -6 to 6
Outputs:
- merged: float32 [8192, 1024], P('row', 'col')
The draws below stay inside these ranges and needn't reach their ends.
All inputs are finite; a program needn't handle non-finite values.
Results may differ from the reference program's by a relative error of at most 0.0045.
Values may be sent and summed in bfloat16 or wider, within the bound.
A program may use at most 128 MiB of HBM per device.

```python
import jax
import jax.numpy as jnp
from jax import lax

D = 8192
DOUT = 1024
MEMBERS = 4
ITERS = 3
TOK = 1024


def feature_layout(key):
    base_key = jax.random.fold_in(key, 9173)
    feature_rank = jax.random.permutation(jax.random.fold_in(base_key, 1), D)
    loud_count = max(4, D // 1024)
    loud_mask = feature_rank < loud_count
    loud_level = jax.random.uniform(jax.random.fold_in(base_key, 2), (D,), jnp.float32, 3.5, 6.0)
    return (loud_mask, loud_level)


def column_layout(key):
    base_key = jax.random.fold_in(key, 9181)
    column_rank = jax.random.permutation(jax.random.fold_in(base_key, 1), DOUT)
    hot_count = max(2, DOUT // 128)
    return column_rank < hot_count


def draw_activations(key, part):
    loud_mask, loud_level = feature_layout(key)
    own_key = jax.random.fold_in(key, 11)
    full_shape = (MEMBERS, TOK, D)
    bulk_values = jnp.clip(jax.random.normal(jax.random.fold_in(own_key, 2), full_shape, jnp.float32), -6.0, 6.0)
    magnitude = jax.random.uniform(jax.random.fold_in(own_key, 3), full_shape, jnp.float32, 0.6, 1.0)
    sign_values = jnp.where(jax.random.bernoulli(jax.random.fold_in(own_key, 4), 0.5, full_shape), 1.0, -1.0)
    loud_values = sign_values * magnitude * loud_level
    return jnp.where(loud_mask[None, None, :], loud_values, bulk_values).astype(jnp.bfloat16)


def draw_member_weights(key, part):
    loud_mask, loud_level = feature_layout(key)
    hot_mask = column_layout(key)
    own_key = jax.random.fold_in(key, 23)
    full_shape = (MEMBERS, D, DOUT)
    bulk_values = jnp.clip(jax.random.normal(jax.random.fold_in(own_key, 2), full_shape, jnp.float32), -6.0, 6.0)
    magnitude = jax.random.uniform(jax.random.fold_in(own_key, 3), full_shape, jnp.float32, 3.0, 6.0)
    sign_values = jnp.where(jax.random.bernoulli(jax.random.fold_in(own_key, 4), 0.5, full_shape), 1.0, -1.0)
    hot_values = sign_values * magnitude
    cold_values = 0.1 * bulk_values
    loud_rows = jnp.where(hot_mask[None, None, :], hot_values, cold_values)
    return jnp.where(loud_mask[None, :, None], loud_rows, bulk_values).astype(jnp.bfloat16)


def setup_inputs(seed: int = 0) -> dict:
    arg_keys = jax.random.split(jax.random.key(seed), 3)
    return {
        "activations": draw_activations(jax.random.fold_in(arg_keys[2], 71), 0),
        "member_weights": draw_member_weights(jax.random.fold_in(arg_keys[2], 71), 0),
    }


BLEND_WEIGHT = 0.9


def apply_system(activations, diag_all, vector):
    result_sum = jnp.zeros(vector.shape, jnp.float32)
    for member in range(MEMBERS):
        member_acts = activations[member].astype(jnp.float32)
        projected = jnp.dot(member_acts, vector, precision=lax.Precision.HIGHEST, preferred_element_type=jnp.float32)
        back_proj = lax.dot_general(member_acts, projected, (((0,), (0,)), ((), ())), precision=lax.Precision.HIGHEST, preferred_element_type=jnp.float32)
        result_sum = result_sum + BLEND_WEIGHT * back_proj / TOK + (1.0 - BLEND_WEIGHT) * diag_all[member][:, None] * vector
    return result_sum


def reference(activations, member_weights):
    slab_width = min(D, 512)
    column_ids = jnp.arange(D, dtype=jnp.int32)

    def rhs_block(block_index):
        first_row = block_index * slab_width
        row_ids = first_row + jnp.arange(slab_width, dtype=jnp.int32)
        factor = jnp.where(row_ids[:, None] == column_ids[None, :], jnp.float32(1.0), jnp.float32(BLEND_WEIGHT))
        accum = jnp.zeros((slab_width, DOUT), jnp.float32)
        for member in range(MEMBERS):
            member_acts = activations[member]
            row_slab = lax.dynamic_slice_in_dim(member_acts, first_row, slab_width, 1)
            gram_rows = lax.dot_general(row_slab, member_acts, (((0,), (0,)), ((), ())), preferred_element_type=jnp.float32) / TOK
            scaled_low = (gram_rows * factor).astype(jnp.bfloat16)
            accum = accum + jnp.dot(scaled_low, member_weights[member], preferred_element_type=jnp.float32)
        return accum

    right_side = lax.map(rhs_block, jnp.arange(D // slab_width, dtype=jnp.int32)).reshape(D, DOUT)
    acts_wide = activations.astype(jnp.float32)
    diag_all = jnp.sum(acts_wide * acts_wide, axis=1) / TOK
    merged = jnp.zeros((D, DOUT), jnp.float32)
    residual = right_side
    direction = right_side
    norm_now = jnp.sum(residual * residual)
    for iteration in range(ITERS):
        image_out = apply_system(activations, diag_all, direction)
        step_size = norm_now / jnp.sum(direction * image_out)
        merged = merged + step_size * direction
        residual = residual - step_size * image_out
        norm_next = jnp.sum(residual * residual)
        direction = residual + (norm_next / norm_now) * direction
        norm_now = norm_next
    return merged
```

```python
import jax
import jax.numpy as jnp
from jax import lax
from jax.sharding import PartitionSpec as P

ITERS = 3
BLEND_WEIGHT = 0.9


def local(activations, member_weights):
    rows = lax.axis_size("row")
    cols = lax.axis_size("col")
    per = rows // cols
    row_index = lax.axis_index("row")
    members, tok_block, width = activations.shape
    tokens = tok_block * cols
    out_group = member_weights.shape[2] // cols
    sub = member_weights.shape[1]
    low = jnp.bfloat16

    acts = lax.all_gather(activations, "col", axis=1, tiled=True)
    flat = acts.reshape(members * tokens, width)
    pieces = member_weights.reshape(members, sub, cols, out_group).transpose(2, 0, 1, 3)
    pieces = lax.all_to_all(pieces, "col", 0, 0, tiled=True)
    half = row_index // cols
    slots = jnp.zeros((cols, per) + pieces.shape[1:], low)
    slots = jnp.where(
        lax.broadcasted_iota(jnp.int32, slots.shape, 1) == half, pieces[:, None], slots
    ).reshape((rows,) + pieces.shape[1:])
    got = lax.all_to_all(slots, "row", 0, 0, tiled=True)
    got = got.reshape((per, cols) + pieces.shape[1:])
    got = jnp.where(row_index % per == 0, got[0], got[1])
    weights = got.transpose(1, 0, 2, 3).reshape(members, width, out_group)

    wide = acts.astype(jnp.float32)
    diag = jnp.sum(wide * wide, axis=1) * ((1.0 - BLEND_WEIGHT) / tokens)
    diag_sum = jnp.sum(diag, axis=0)[:, None]
    scale = BLEND_WEIGHT / tokens

    def back(partial):
        share = lax.psum_scatter(partial, "row", scatter_dimension=0, tiled=True)
        full = lax.all_gather(share.astype(low), "row", axis=0, tiled=True)
        return scale * lax.dot_general(
            flat, full, (((0,), (0,)), ((), ())), preferred_element_type=jnp.float32
        )

    def total(*terms):
        return lax.psum(jnp.stack([jnp.sum(a * b) for a, b in terms]), ("row", "col"))

    first = jnp.einsum("mtf,mfd->mtd", acts, weights, preferred_element_type=jnp.float32)
    right_side = back(first.reshape(members * tokens, out_group)) + jnp.sum(
        diag[:, :, None] * weights.astype(jnp.float32), axis=0
    )

    merged = jnp.zeros_like(right_side)
    residual = right_side
    direction = right_side
    norm_now = None
    for iteration in range(ITERS):
        shadow = direction.astype(low)
        partial = jnp.dot(flat, shadow, preferred_element_type=jnp.float32)
        image = back(partial) + diag_sum * direction
        if iteration == 0:
            norm_now, along = total((residual, residual), (direction, image))
        else:
            (along,) = total((direction, image))
        step = norm_now / along
        merged = merged + step * direction
        if iteration + 1 < ITERS:
            residual = residual - step * image
            (norm_next,) = total((residual, residual))
            direction = residual + (norm_next / norm_now) * direction
            norm_now = norm_next
    return merged


def solution(mesh):
    return jax.shard_map(
        local,
        mesh=mesh,
        in_specs=(P(None, "col", "row"), P(None, ("col", "row"), None)),
        out_specs=P("row", "col"),
        check_vma=False,
    )
```

```python
import jax
import jax.numpy as jnp
from jax import lax
from jax.experimental import pallas as pl
from jax.experimental.pallas import tpu as pltpu
from jax.sharding import PartitionSpec as P

ITERS = 3
BLEND_WEIGHT = 0.9
LOW = jnp.bfloat16
WIDE = jnp.float32
MESH = pl.DeviceIdType.MESH


def dot_nt(a, b):
    return lax.dot_general(a, b, (((1,), (1,)), ((), ())), preferred_element_type=WIDE)


def dot_nn(a, b):
    return lax.dot_general(a, b, (((1,), (0,)), ((), ())), preferred_element_type=WIDE)


def fold(v):
    rows, lanes = v.shape
    v = jnp.sum(v.reshape(rows // 8, 8, lanes), axis=0)
    out = v[:, 0:128]
    for i in range(1, lanes // 128):
        out = out + v[:, 128 * i : 128 * (i + 1)]
    return out


def kernel(
    acts, wts, out,
    xb, wb, wt, dacc, dsum, v, own, psend, precv, pacc, asend, arecv, acc, r, d, x, ex, tile, sa, tile2, sb,
    lsem, xs_sem, xr_sem, fs_sem, fr_sem, ws_sem, wr_sem, wfs_sem, wfr_sem,
    rs_s, rs_r, ag_s, ag_r, s1_s, s1_r, s2_s, s2_r, ex_s, ex_r,
):
    groups, cols = 8, 8
    members, tok = acts.shape[0], acts.shape[1]
    width = acts.shape[2]
    part = v.shape[1]
    scale = BLEND_WEIGHT / (tok * cols)
    dscale = (1.0 - BLEND_WEIGHT) / (tok * cols)

    row = lax.axis_index("row")
    col = lax.axis_index("col")
    g = row // 2
    k = row % 2
    z = col // 2
    y = col % 2
    q = col * 2 + k

    def copy(src, dst, ss, rs, to_row, to_col):
        return pltpu.make_async_remote_copy(
            src_ref=src, dst_ref=dst, send_sem=ss, recv_sem=rs,
            device_id=(to_row, to_col), device_id_type=MESH,
        )

    barrier = pltpu.get_barrier_semaphore()

    def greet(to_row, to_col):
        pl.semaphore_signal(barrier, inc=1, device_id=(to_row, to_col), device_id_type=MESH)

    @pl.loop(1, groups)
    def _(i):
        greet(((g + i) % groups) * 2 + k, col)

    @pl.loop(1, 2 * cols)
    def _(i):
        p = (q + i) % (2 * cols)
        greet(2 * g + p % 2, p // 2)

    @pl.loop(0, cols)
    def _(i):
        @pl.when(jnp.logical_or(col != g, i != col))
        def _():
            greet(2 * col + k, i)

        @pl.when(jnp.logical_or(col != g, i != g))
        def _():
            greet(2 * i + k, g)

    @pl.when(col == g)
    def _():
        pl.semaphore_wait(barrier, 7 + 15 + 14)

    @pl.when(col != g)
    def _():
        pl.semaphore_wait(barrier, 7 + 15 + 16)

    zp = ((z + 1) % 4) * 2
    zm = ((z + 3) % 4) * 2
    zf = ((z + 2) % 4) * 2
    yo = 1 - y
    b_y, b_m, b_p = z * 2 + yo, zm + y, zp + y
    b_my, b_py, b_f, b_fy = zm + yo, zp + yo, zf + y, zf + yo
    c_y, c_p, c_m = z * 2 + yo, zp + y, zm + y
    half = members // 2
    lo, hi = pl.ds(0, half), pl.ds(half, half)
    other = 2 * g + 1 - k

    sends = []

    def start(c):
        c.start()
        sends.append(c)

    def forward(block, n, ms=None):
        ref = xb.at[k, block] if ms is None else xb.at[k, block, ms]
        start(copy(ref, ref, fs_sem.at[n], fr_sem.at[n], other, col))

    local_x = pltpu.make_async_copy(acts, xb.at[k, col], lsem.at[0])
    local_x.start()
    mine = xb.at[k, col]
    start(copy(acts, mine, xs_sem.at[0], xr_sem.at[0], row, c_y))
    start(copy(acts, mine, xs_sem.at[1], xr_sem.at[1], row, c_p))
    start(copy(acts, mine, xs_sem.at[2], xr_sem.at[2], row, c_m))
    start(copy(acts, mine, fs_sem.at[9], fr_sem.at[9], other, col))

    def wcopy(i):
        return copy(
            wts.at[:, :, pl.ds(pl.multiple_of(i * 128, 128), 128)], wb.at[row],
            ws_sem.at[i], wr_sem.at[g], 2 * col + k, i,
        )

    def wlocal():
        return pltpu.make_async_copy(
            wts.at[:, :, pl.ds(pl.multiple_of(col * 128, 128), 128)], wb.at[row], lsem.at[1]
        )

    @pl.loop(0, cols)
    def _(i):
        me = jnp.logical_and(col == g, i == col)

        @pl.when(me)
        def _():
            wlocal().start()

        @pl.when(jnp.logical_not(me))
        def _():
            wcopy(i).start()

    def diag(h, j, first=False):
        for m in range(members):
            t = xb[h, j, m].astype(WIDE)
            t = jnp.sum((t * t).reshape(tok // 8, 8, width), axis=0)
            if first:
                dacc[h, m] = t
            else:
                dacc[h, m] = dacc[h, m] + t

    local_x.wait()

    def fwait(n, block, ms=None):
        ref = xb.at[1 - k, block] if ms is None else xb.at[1 - k, block, ms]
        copy(ref, ref, fs_sem.at[n], fr_sem.at[n], other, col).wait_recv()

    def xwait(n, block, ms=None):
        ref = xb.at[k, block] if ms is None else xb.at[k, block, ms]
        copy(ref, ref, xs_sem.at[0], xr_sem.at[n], row, c_y).wait_recv()

    fwait(9, col)
    diag(0, col, True)
    diag(1, col, True)

    @pl.loop(0, groups)
    def _(i):
        src = 2 * i + k
        me = jnp.logical_and(col == g, i == g)

        @pl.when(me)
        def _():
            wlocal().wait()

        @pl.when(jnp.logical_not(me))
        def _():
            copy(wb.at[src], wb.at[src], ws_sem.at[0], wr_sem.at[i], row, c_y).wait_recv()

        copy(wb.at[src], wb.at[src], wfs_sem.at[i], wfr_sem.at[i], other, col).start()

    @pl.loop(0, groups)
    def _(i):
        src = 2 * i + 1 - k
        copy(wb.at[src], wb.at[src], wfs_sem.at[i], wfr_sem.at[i], other, col).wait_recv()

    for h in range(2):
        for m in range(members):
            w = wb[8 * h : 8 * h + 8, m].reshape(width, 2 * part)
            wt[m, h] = jnp.transpose(w.astype(WIDE)).astype(LOW)

    kpart = pl.ds(pl.multiple_of(k * part, part), part)

    def rs_copy(a, i):
        return copy(
            psend.at[a, i - 1], precv.at[a, i - 1], rs_s.at[a], rs_r.at[a],
            ((g + i) % groups) * 2 + k, col,
        )

    def first_chunk(j):
        i = (j + groups - g) % groups
        for m in range(members):
            t = dot_nt(wt[m, 0, kpart, :], xb[0, j, m]) + dot_nt(wt[m, 1, kpart, :], xb[1, j, m])
            own[:, m * tok : (m + 1) * tok] = t

        @pl.when(j == g)
        def _():
            pacc[...] = own[...]

        @pl.when(j != g)
        def _():
            psend[0, i - 1] = own[...].astype(LOW)
            rs_copy(0, i).start()

    first_chunk(col)

    xwait(0, b_y)
    start(copy(xb.at[k, b_y], xb.at[k, b_y], xs_sem.at[3], xr_sem.at[3], row, c_p))
    start(copy(xb.at[k, b_y], xb.at[k, b_y], xs_sem.at[4], xr_sem.at[4], row, c_m))
    forward(b_y, 0)
    xwait(1, b_m)
    start(copy(xb.at[k, b_m, lo], xb.at[k, b_m, lo], xs_sem.at[5], xr_sem.at[5], row, c_p))
    forward(b_m, 1)
    xwait(2, b_p)
    start(copy(xb.at[k, b_p, hi], xb.at[k, b_p, hi], xs_sem.at[6], xr_sem.at[6], row, c_m))
    forward(b_p, 2)
    for n, b in ((0, b_y), (1, b_m), (2, b_p)):
        fwait(n, b)
        diag(0, b)
        diag(1, b)
        first_chunk(b)
    xwait(5, b_f, lo)
    start(copy(xb.at[k, b_f, lo], xb.at[k, b_f, lo], xs_sem.at[7], xr_sem.at[7], row, c_y))
    forward(b_f, 5, lo)
    xwait(6, b_f, hi)
    start(copy(xb.at[k, b_f, hi], xb.at[k, b_f, hi], xs_sem.at[8], xr_sem.at[8], row, c_y))
    forward(b_f, 6, hi)
    xwait(3, b_my)
    forward(b_my, 3)
    xwait(4, b_py)
    forward(b_py, 4)
    fwait(5, b_f, lo)
    fwait(6, b_f, hi)
    diag(0, b_f)
    diag(1, b_f)
    first_chunk(b_f)
    for n, b in ((3, b_my), (4, b_py)):
        fwait(n, b)
        diag(0, b)
        diag(1, b)
        first_chunk(b)
    xwait(7, b_fy, lo)
    forward(b_fy, 7, lo)
    xwait(8, b_fy, hi)
    forward(b_fy, 8, hi)
    fwait(7, b_fy, lo)
    fwait(8, b_fy, hi)
    diag(0, b_fy)
    diag(1, b_fy)
    first_chunk(b_fy)

    for h in range(2):
        rhs = None
        total = None
        for m in range(members):
            line = jnp.sum(dacc[h, m], axis=0, keepdims=True) * dscale
            term = line * wt[m, h, kpart, :].astype(WIDE)
            rhs = term if rhs is None else rhs + term
            total = line if total is None else total + line
        r[h] = rhs
        dsum[h] = jnp.broadcast_to(total, (8, width))

    def rs_wait(a):
        copy(precv.at[a], precv.at[a], rs_s.at[a], rs_r.at[a], row, c_y).wait_recv()

    def rs_total(a):
        s = precv[a, 0].astype(WIDE)
        for i in range(1, groups - 1):
            s = s + precv[a, i].astype(WIDE)
        return s

    def ag_copy(a, i):
        return copy(
            asend.at[a], arecv.at[a, i - 1], ag_s.at[a, i - 1], ag_r.at[a, i - 1],
            ((g + i) % groups) * 2 + k, col,
        )

    def ag_start(a):
        @pl.loop(1, groups)
        def _(i):
            ag_copy(a, i).start()

    def back_own(a):
        for h in range(2):
            acc[h] = dot_nn(asend[a], xb[h, g].reshape(members * tok, width))

    def back_rest(a):
        @pl.loop(1, groups)
        def _(i):
            j = (g + groups - i) % groups
            ag_copy(a, i).wait_recv()
            p = arecv[a, i - 1]
            for h in range(2):
                acc[h] = acc[h] + dot_nn(p, xb[h, j].reshape(members * tok, width))

    def forth(a):
        def chunk(j):
            return dot_nt(v[0], xb[0, j].reshape(members * tok, width)) + dot_nt(
                v[1], xb[1, j].reshape(members * tok, width)
            )

        @pl.loop(1, groups)
        def _(i):
            psend[a, i - 1] = chunk((g + i) % groups).astype(LOW)
            rs_copy(a, i).start()

        own[...] = chunk(g)

    def s1_copy(e, i):
        return copy(
            tile.at[e], sa.at[e, i - 1], s1_s.at[e, i - 1], s1_r.at[e], ((g + i) % groups) * 2 + k, col
        )

    def s1_start(e):
        @pl.loop(1, groups)
        def _(i):
            s1_copy(e, i).start()

    def s2_copy(e, i):
        p = (q + i) % (2 * cols)
        return copy(
            tile2.at[e], sb.at[e, i - 1], s2_s.at[e, i - 1], s2_r.at[e], 2 * g + p % 2, p // 2
        )

    def s1_finish(e):
        copy(sa.at[e], sa.at[e], s1_s.at[e, 0], s1_r.at[e], row, c_y).wait_recv()
        s = tile[e]
        for i in range(groups - 1):
            s = s + sa[e, i]
        tile2[e] = s

        @pl.loop(1, 2 * cols)
        def _(i):
            s2_copy(e, i).start()

    def s2_finish(e):
        copy(sb.at[e], sb.at[e], s2_s.at[e, 0], s2_r.at[e], row, c_y).wait_recv()
        s = tile2[e]
        for i in range(2 * cols - 1):
            s = s + sb[e, i]
        return s

    rs_wait(0)
    asend[0] = (pacc[...] + rs_total(0)).astype(LOW)
    ag_start(0)
    back_own(0)
    back_rest(0)
    for h in range(2):
        r[h] = r[h] + scale * acc[h]
        d[h] = r[h]
        v[h] = r[h].astype(LOW)
        x[h] = jnp.zeros_like(r[h])

    rr = None
    for it in range(ITERS):
        a = it + 1
        forth(a)
        beta = None
        if it > 0:
            e = 2 * it - 1
            s1_finish(e)
            new = jnp.sum(s2_finish(e)[0])
            beta = new / rr
            rr = new
            for h in range(2):
                d[h] = r[h] + beta * d[h]
        if it == ITERS - 1:
            for n, ref in ((0, x), (1, d)):
                start(copy(ref.at[1 - k], ex.at[n], ex_s.at[n], ex_r.at[n], other, col))
        along = None
        norm = None
        for h in range(2):
            t = fold(d[h] * d[h] * dsum[h, 0:1])
            along = t if along is None else along + t
            if it == 0:
                t = fold(r[h] * r[h])
                norm = t if norm is None else norm + t
        rs_wait(a)
        p = own[...] + rs_total(a)
        if it > 0:
            p = p + beta * pacc[...]
        pacc[...] = p
        e = 2 * it
        if it < ITERS - 1:
            asend[a] = p.astype(LOW)
            ag_start(a)
        tile[e, 0] = along + scale * fold(p * p)
        tile[e, 1] = along if norm is None else norm
        s1_start(e)
        if it < ITERS - 1:
            back_own(a)
        s1_finish(e)
        if it < ITERS - 1:
            back_rest(a)
        s = s2_finish(e)
        if it == 0:
            rr = jnp.sum(s[1])
        alpha = rr / jnp.sum(s[0])
        if it < ITERS - 1:
            norm = None
            for h in range(2):
                image = scale * acc[h] + dsum[h, 0:1] * d[h]
                x[h] = x[h] + alpha * d[h]
                rh = r[h] - alpha * image
                r[h] = rh
                v[h] = rh.astype(LOW)
                t = fold(rh * rh)
                norm = t if norm is None else norm + t
            e = 2 * it + 1
            tile[e, 0] = norm
            tile[e, 1] = norm
            s1_start(e)
        else:
            for n in range(2):
                copy(ex.at[n], ex.at[n], ex_s.at[n], ex_r.at[n], other, col).wait_recv()
            mine_part = x[k] + alpha * d[k]
            other_part = ex[0] + alpha * ex[1]

            @pl.when(k == 0)
            def _():
                out[...] = jnp.transpose(jnp.concatenate([mine_part, other_part], axis=0))

            @pl.when(k == 1)
            def _():
                out[...] = jnp.transpose(jnp.concatenate([other_part, mine_part], axis=0))

    for c in sends:
        c.wait_send()

    @pl.loop(0, cols)
    def _(i):
        @pl.when(jnp.logical_or(col != g, i != col))
        def _():
            wcopy(i).wait_send()

        copy(wb.at[0], wb.at[0], wfs_sem.at[i], wfr_sem.at[i], other, col).wait_send()

    for a in range(ITERS + 1):
        copy(psend.at[a], psend.at[a], rs_s.at[a], rs_r.at[a], row, c_y).wait_send()

    @pl.loop(1, groups)
    def _(i):
        for a in range(ITERS):
            ag_copy(a, i).wait_send()
        for e in range(2 * ITERS - 1):
            s1_copy(e, i).wait_send()

    @pl.loop(1, 2 * cols)
    def _(i):
        for e in range(2 * ITERS - 1):
            s2_copy(e, i).wait_send()


def local(acts, wts):
    members, tok, width = acts.shape
    cols = lax.axis_size("col")
    groups = lax.axis_size("row") // 2
    part = wts.shape[2] // (2 * cols)
    apps = ITERS + 1
    events = 2 * ITERS - 1
    chunk = members * tok
    vmem = pltpu.VMEM
    dma = pltpu.SemaphoreType.DMA
    return pl.pallas_call(
        kernel,
        out_shape=jax.ShapeDtypeStruct((width, 2 * part), WIDE),
        in_specs=[pl.BlockSpec(memory_space=pl.ANY)] * 2,
        out_specs=pl.BlockSpec(memory_space=pltpu.VMEM),
        scratch_shapes=[
            vmem((2, cols, members, tok, width), LOW),
            vmem((2 * groups, members, wts.shape[1], 2 * part), LOW),
            vmem((members, 2, 2 * part, width), LOW),
            vmem((2, members, 8, width), WIDE),
            vmem((2, 8, width), WIDE),
            vmem((2, part, width), LOW),
            vmem((part, chunk), WIDE),
            vmem((apps, groups - 1, part, chunk), LOW),
            vmem((apps, groups - 1, part, chunk), LOW),
            vmem((part, chunk), WIDE),
            vmem((ITERS, part, chunk), LOW),
            vmem((ITERS, groups - 1, part, chunk), LOW),
            vmem((2, part, width), WIDE),
            vmem((2, part, width), WIDE),
            vmem((2, part, width), WIDE),
            vmem((2, part, width), WIDE),
            vmem((2, part, width), WIDE),
            vmem((events, 2, 8, 128), WIDE),
            vmem((events, groups - 1, 2, 8, 128), WIDE),
            vmem((events, 2, 8, 128), WIDE),
            vmem((events, 2 * cols - 1, 2, 8, 128), WIDE),
            dma((2,)),
            dma((9,)),
            dma((9,)),
            dma((10,)),
            dma((10,)),
            dma((cols,)),
            dma((cols,)),
            dma((cols,)),
            dma((cols,)),
            dma((apps,)),
            dma((apps,)),
            dma((ITERS, groups - 1)),
            dma((ITERS, groups - 1)),
            dma((events, groups - 1)),
            dma((events,)),
            dma((events, 2 * cols - 1)),
            dma((events,)),
            dma((2,)),
            dma((2,)),
        ],
        compiler_params=pltpu.CompilerParams(
            collective_id=0, has_side_effects=True, vmem_limit_bytes=60 << 20
        ),
        name="regmean_cg",
    )(acts, wts)


def solution(mesh):
    return jax.shard_map(
        local,
        mesh=mesh,
        in_specs=(P(None, "col", "row"), P(None, ("col", "row"), None)),
        out_specs=P("row", "col"),
        check_vma=False,
    )
```

```python
import jax
import jax.numpy as jnp
from jax import lax
from jax.experimental import pallas as pl
from jax.experimental.pallas import tpu as pltpu
from jax.sharding import PartitionSpec as P

ITERS = 3
BLEND_WEIGHT = 0.9
LOW = jnp.bfloat16
WIDE = jnp.float32
MESH = pl.DeviceIdType.MESH


def dot_nt(a, b):
    return lax.dot_general(a, b, (((1,), (1,)), ((), ())), preferred_element_type=WIDE)


def dot_nn(a, b):
    return lax.dot_general(a, b, (((1,), (0,)), ((), ())), preferred_element_type=WIDE)


def fold(v):
    rows, lanes = v.shape
    v = jnp.sum(v.reshape(rows // 8, 8, lanes), axis=0)
    out = v[:, 0:128]
    for i in range(1, lanes // 128):
        out = out + v[:, 128 * i : 128 * (i + 1)]
    return out


def kernel(
    acts, wts, out,
    xb, w1, wb, wt, dacc, dsum, v, own, psend, precv, pacc, asend, arecv, acc, r, d, x, ex, tile, sa, tile2, sb,
    lsem, xs_sem, xr_sem, fs_sem, fr_sem, w1_s, w1_r, w2_s, w2_r, w3_s, w3_r,
    rs_s, rs_r, ag_s, ag_r, s1_s, s1_r, s2_s, s2_r, ex_s, ex_r,
):
    groups, cols = 8, 8
    members, tok = acts.shape[0], acts.shape[1]
    width = acts.shape[2]
    part = v.shape[1]
    scale = BLEND_WEIGHT / (tok * cols)
    dscale = (1.0 - BLEND_WEIGHT) / (tok * cols)

    row = lax.axis_index("row")
    col = lax.axis_index("col")
    g = row // 2
    k = row % 2
    x4 = g % 4
    y2 = g // 4
    z = col // 2
    y = col % 2
    q = col * 2 + k

    def copy(src, dst, ss, rs, to_row, to_col):
        return pltpu.make_async_remote_copy(
            src_ref=src, dst_ref=dst, send_sem=ss, recv_sem=rs,
            device_id=(to_row, to_col), device_id_type=MESH,
        )

    def peer(i):
        return ((y2 + i // 4) % 2) * 4 + (x4 + i) % 4

    def source(i):
        return ((y2 + i // 4) % 2) * 4 + (x4 + 4 - i % 4) % 4

    barrier = pltpu.get_barrier_semaphore()

    def greet(to_row, to_col):
        pl.semaphore_signal(barrier, inc=1, device_id=(to_row, to_col), device_id_type=MESH)

    @pl.loop(1, groups)
    def _(i):
        greet(peer(i) * 2 + k, col)

    @pl.loop(1, 2 * cols)
    def _(i):
        p = (q + i) % (2 * cols)
        greet(2 * g + p % 2, p // 2)

    pl.semaphore_wait(barrier, 7 + 15)

    zp = ((z + 1) % 4) * 2
    zm = ((z + 3) % 4) * 2
    zf = ((z + 2) % 4) * 2
    yo = 1 - y
    b_y, b_m, b_p = z * 2 + yo, zm + y, zp + y
    b_my, b_py, b_f, b_fy = zm + yo, zp + yo, zf + y, zf + yo
    c_y, c_p, c_m = z * 2 + yo, zp + y, zm + y
    half = members // 2
    lo, hi = pl.ds(0, half), pl.ds(half, half)
    other = 2 * g + 1 - k

    sends = []

    def start(c):
        c.start()
        sends.append(c)

    def forward(block, n, ms=None):
        ref = xb.at[k, block] if ms is None else xb.at[k, block, ms]
        start(copy(ref, ref, fs_sem.at[n], fr_sem.at[n], other, col))

    def w1_src(c):
        return wts.at[:, :, pl.ds(pl.multiple_of(c * 128, 128), 128)]

    def w1_copy(i):
        c = ((z + i // 2) % 4) * 2 + (y + i) % 2
        return copy(w1_src(c), w1.at[col], w1_s.at[i], w1_r.at[i], row, c)

    def w1_from(i):
        return ((z + 4 - i // 2) % 4) * 2 + (y + i) % 2

    local_w = pltpu.make_async_copy(w1_src(col), w1.at[col], lsem.at[1])
    local_w.start()

    @pl.loop(1, cols)
    def _(n):
        w1_copy(cols - n).start()

    local_x = pltpu.make_async_copy(acts, xb.at[k, col], lsem.at[0])
    local_x.start()
    mine = xb.at[k, col]
    start(copy(acts, mine, xs_sem.at[0], xr_sem.at[0], row, c_y))
    start(copy(acts, mine, xs_sem.at[1], xr_sem.at[1], row, c_p))
    start(copy(acts, mine, xs_sem.at[2], xr_sem.at[2], row, c_m))
    start(copy(acts, mine, fs_sem.at[9], fr_sem.at[9], other, col))

    def diag(h, j, first=False):
        for m in range(members):
            t = xb[h, j, m].astype(WIDE)
            t = jnp.sum((t * t).reshape(tok // 8, 8, width), axis=0)
            if first:
                dacc[h, m] = t
            else:
                dacc[h, m] = dacc[h, m] + t

    local_x.wait()

    def fwait(n, block, ms=None):
        ref = xb.at[1 - k, block] if ms is None else xb.at[1 - k, block, ms]
        copy(ref, ref, fs_sem.at[n], fr_sem.at[n], other, col).wait_recv()

    def xwait(n, block, ms=None):
        ref = xb.at[k, block] if ms is None else xb.at[k, block, ms]
        copy(ref, ref, xs_sem.at[0], xr_sem.at[n], row, c_y).wait_recv()

    def relay(n, block, to, ms=None):
        ref = xb.at[k, block] if ms is None else xb.at[k, block, ms]
        start(copy(ref, ref, xs_sem.at[n], xr_sem.at[n], row, to))

    def w2_copy(i):
        p = peer(i)
        return copy(w1.at[p], wb.at[row], w2_s.at[i], w2_r.at[i], 2 * p + k, col)

    def w2_forward(i):
        ref = wb.at[2 * source(i) + k]
        return copy(ref, ref, w3_s.at[i], w3_r.at[i], other, col)

    local_w.wait()

    @pl.loop(1, cols)
    def _(n):
        i = cols - n
        ref = w1.at[w1_from(i)]
        copy(ref, ref, w1_s.at[i], w1_r.at[i], row, c_y).wait_recv()

    @pl.loop(1, groups)
    def _(n):
        w2_copy(groups - n).start()

    own_w = pltpu.make_async_copy(w1.at[g], wb.at[row], lsem.at[1])
    own_w.start()
    fwait(9, col)
    diag(0, col, True)
    diag(1, col, True)
    own_w.wait()
    w2_forward(0).start()
    xwait(1, b_m)
    relay(5, b_m, c_p, lo)
    forward(b_m, 1)
    xwait(2, b_p)
    relay(6, b_p, c_m, hi)
    forward(b_p, 2)
    xwait(0, b_y)
    relay(3, b_y, c_p)
    relay(4, b_y, c_m)
    forward(b_y, 0)

    @pl.loop(1, groups)
    def _(n):
        i = groups - n
        ref = wb.at[2 * source(i) + k]
        copy(ref, ref, w2_s.at[i], w2_r.at[i], row, c_y).wait_recv()
        w2_forward(i).start()

    @pl.loop(0, groups)
    def _(i):
        ref = wb.at[2 * source(i) + 1 - k]
        copy(ref, ref, w3_s.at[i], w3_r.at[i], other, col).wait_recv()

    for h in range(2):
        for m in range(members):
            w = wb[8 * h : 8 * h + 8, m].reshape(width, 2 * part)
            wt[m, h] = jnp.transpose(w.astype(WIDE)).astype(LOW)

    kpart = pl.ds(pl.multiple_of(k * part, part), part)

    def rs_copy(a, i):
        return copy(
            psend.at[a, i - 1], precv.at[a, i - 1], rs_s.at[a], rs_r.at[a],
            peer(i) * 2 + k, col,
        )

    def first_chunk(j):
        i = ((j // 4 + y2) % 2) * 4 + (j + 4 - x4) % 4
        for m in range(members):
            t = dot_nt(wt[m, 0, kpart, :], xb[0, j, m]) + dot_nt(wt[m, 1, kpart, :], xb[1, j, m])
            own[:, m * tok : (m + 1) * tok] = t

        @pl.when(j == g)
        def _():
            pacc[...] = own[...]

        @pl.when(j != g)
        def _():
            psend[0, i - 1] = own[...].astype(LOW)
            rs_copy(0, i).start()

    def use(block):
        first_chunk(block)
        diag(0, block)
        diag(1, block)

    first_chunk(col)
    for n, b in ((0, b_y), (1, b_m), (2, b_p)):
        fwait(n, b)
        use(b)
    xwait(5, b_f, lo)
    relay(7, b_f, c_y, lo)
    forward(b_f, 5, lo)
    xwait(6, b_f, hi)
    relay(8, b_f, c_y, hi)
    forward(b_f, 6, hi)
    fwait(5, b_f, lo)
    fwait(6, b_f, hi)
    use(b_f)
    xwait(3, b_my)
    forward(b_my, 3)
    xwait(4, b_py)
    forward(b_py, 4)
    xwait(7, b_fy, lo)
    forward(b_fy, 7, lo)
    xwait(8, b_fy, hi)
    forward(b_fy, 8, hi)
    fwait(3, b_my)
    use(b_my)
    fwait(4, b_py)
    use(b_py)
    fwait(7, b_fy, lo)
    fwait(8, b_fy, hi)
    use(b_fy)

    for h in range(2):
        rhs = None
        total = None
        for m in range(members):
            line = jnp.sum(dacc[h, m], axis=0, keepdims=True) * dscale
            term = line * wt[m, h, kpart, :].astype(WIDE)
            rhs = term if rhs is None else rhs + term
            total = line if total is None else total + line
        r[h] = rhs
        dsum[h] = jnp.broadcast_to(total, (8, width))

    def rs_wait(a):
        copy(precv.at[a], precv.at[a], rs_s.at[a], rs_r.at[a], row, c_y).wait_recv()

    def rs_total(a):
        s = precv[a, 0].astype(WIDE)
        for i in range(1, groups - 1):
            s = s + precv[a, i].astype(WIDE)
        return s

    def ag_copy(a, i):
        return copy(
            asend.at[a], arecv.at[a, i - 1], ag_s.at[a, i - 1], ag_r.at[a, i - 1],
            peer(i) * 2 + k, col,
        )

    def ag_start(a):
        @pl.loop(1, groups)
        def _(n):
            ag_copy(a, groups - n).start()

    def back_own(a):
        for h in range(2):
            acc[h] = dot_nn(asend[a], xb[h, g].reshape(members * tok, width))

    def back_rest(a):
        @pl.loop(1, groups)
        def _(n):
            i = groups - n
            j = source(i)
            ag_copy(a, i).wait_recv()
            p = arecv[a, i - 1]
            for h in range(2):
                acc[h] = acc[h] + dot_nn(p, xb[h, j].reshape(members * tok, width))

    def forth(a):
        def chunk(j):
            return dot_nt(v[0], xb[0, j].reshape(members * tok, width)) + dot_nt(
                v[1], xb[1, j].reshape(members * tok, width)
            )

        @pl.loop(1, groups)
        def _(n):
            i = groups - n
            psend[a, i - 1] = chunk(peer(i)).astype(LOW)
            rs_copy(a, i).start()

        own[...] = chunk(g)

    def s1_copy(e, i):
        return copy(
            tile.at[e], sa.at[e, i - 1], s1_s.at[e, i - 1], s1_r.at[e], peer(i) * 2 + k, col
        )

    def s1_start(e):
        @pl.loop(1, groups)
        def _(i):
            s1_copy(e, i).start()

    def s2_copy(e, i):
        p = (q + i) % (2 * cols)
        return copy(
            tile2.at[e], sb.at[e, i - 1], s2_s.at[e, i - 1], s2_r.at[e], 2 * g + p % 2, p // 2
        )

    def s1_finish(e):
        copy(sa.at[e], sa.at[e], s1_s.at[e, 0], s1_r.at[e], row, c_y).wait_recv()
        s = tile[e]
        for i in range(groups - 1):
            s = s + sa[e, i]
        tile2[e] = s

        @pl.loop(1, 2 * cols)
        def _(i):
            s2_copy(e, i).start()

    def s2_finish(e):
        copy(sb.at[e], sb.at[e], s2_s.at[e, 0], s2_r.at[e], row, c_y).wait_recv()
        s = tile2[e]
        for i in range(2 * cols - 1):
            s = s + sb[e, i]
        return s

    rs_wait(0)
    asend[0] = (pacc[...] + rs_total(0)).astype(LOW)
    ag_start(0)
    back_own(0)
    back_rest(0)
    for h in range(2):
        r[h] = r[h] + scale * acc[h]
        d[h] = r[h]
        v[h] = r[h].astype(LOW)
        x[h] = jnp.zeros_like(r[h])

    rr = None
    for it in range(ITERS):
        a = it + 1
        forth(a)
        beta = None
        if it > 0:
            e = 2 * it - 1
            s1_finish(e)
            new = jnp.sum(s2_finish(e)[0])
            beta = new / rr
            rr = new
            for h in range(2):
                d[h] = r[h] + beta * d[h]
        if it == ITERS - 1:
            for n, ref in ((0, x), (1, d)):
                start(copy(ref.at[1 - k], ex.at[n], ex_s.at[n], ex_r.at[n], other, col))
        along = None
        norm = None
        for h in range(2):
            t = fold(d[h] * d[h] * dsum[h, 0:1])
            along = t if along is None else along + t
            if it == 0:
                t = fold(r[h] * r[h])
                norm = t if norm is None else norm + t
        rs_wait(a)
        p = own[...] + rs_total(a)
        if it > 0:
            p = p + beta * pacc[...]
        pacc[...] = p
        e = 2 * it
        tile[e, 0] = along + scale * fold(p * p)
        tile[e, 1] = along if norm is None else norm
        s1_start(e)
        if it < ITERS - 1:
            asend[a] = p.astype(LOW)
            ag_start(a)
            back_own(a)
        s1_finish(e)
        if it < ITERS - 1:
            back_rest(a)
        s = s2_finish(e)
        if it == 0:
            rr = jnp.sum(s[1])
        alpha = rr / jnp.sum(s[0])
        if it < ITERS - 1:
            norm = None
            for h in range(2):
                image = scale * acc[h] + dsum[h, 0:1] * d[h]
                x[h] = x[h] + alpha * d[h]
                rh = r[h] - alpha * image
                r[h] = rh
                v[h] = rh.astype(LOW)
                t = fold(rh * rh)
                norm = t if norm is None else norm + t
            e = 2 * it + 1
            tile[e, 0] = norm
            tile[e, 1] = norm
            s1_start(e)
        else:
            for n in range(2):
                copy(ex.at[n], ex.at[n], ex_s.at[n], ex_r.at[n], other, col).wait_recv()
            mine_part = x[k] + alpha * d[k]
            other_part = ex[0] + alpha * ex[1]

            @pl.when(k == 0)
            def _():
                out[...] = jnp.transpose(jnp.concatenate([mine_part, other_part], axis=0))

            @pl.when(k == 1)
            def _():
                out[...] = jnp.transpose(jnp.concatenate([other_part, mine_part], axis=0))

    for c in sends:
        c.wait_send()

    @pl.loop(1, cols)
    def _(i):
        w1_copy(i).wait_send()
        w2_copy(i).wait_send()

    @pl.loop(0, groups)
    def _(i):
        w2_forward(i).wait_send()

    for a in range(ITERS + 1):
        copy(psend.at[a], psend.at[a], rs_s.at[a], rs_r.at[a], row, c_y).wait_send()

    @pl.loop(1, groups)
    def _(i):
        for a in range(ITERS):
            ag_copy(a, i).wait_send()
        for e in range(2 * ITERS - 1):
            s1_copy(e, i).wait_send()

    @pl.loop(1, 2 * cols)
    def _(i):
        for e in range(2 * ITERS - 1):
            s2_copy(e, i).wait_send()


def local(acts, wts):
    members, tok, width = acts.shape
    cols = lax.axis_size("col")
    groups = lax.axis_size("row") // 2
    part = wts.shape[2] // (2 * cols)
    apps = ITERS + 1
    events = 2 * ITERS - 1
    chunk = members * tok
    vmem = pltpu.VMEM
    dma = pltpu.SemaphoreType.DMA
    return pl.pallas_call(
        kernel,
        out_shape=jax.ShapeDtypeStruct((width, 2 * part), WIDE),
        in_specs=[pl.BlockSpec(memory_space=pl.ANY)] * 2,
        out_specs=pl.BlockSpec(memory_space=pltpu.VMEM),
        scratch_shapes=[
            vmem((2, cols, members, tok, width), LOW),
            vmem((cols, members, wts.shape[1], 2 * part), LOW),
            vmem((2 * groups, members, wts.shape[1], 2 * part), LOW),
            vmem((members, 2, 2 * part, width), LOW),
            vmem((2, members, 8, width), WIDE),
            vmem((2, 8, width), WIDE),
            vmem((2, part, width), LOW),
            vmem((part, chunk), WIDE),
            vmem((apps, groups - 1, part, chunk), LOW),
            vmem((apps, groups - 1, part, chunk), LOW),
            vmem((part, chunk), WIDE),
            vmem((ITERS, part, chunk), LOW),
            vmem((ITERS, groups - 1, part, chunk), LOW),
            vmem((2, part, width), WIDE),
            vmem((2, part, width), WIDE),
            vmem((2, part, width), WIDE),
            vmem((2, part, width), WIDE),
            vmem((2, part, width), WIDE),
            vmem((events, 2, 8, 128), WIDE),
            vmem((events, groups - 1, 2, 8, 128), WIDE),
            vmem((events, 2, 8, 128), WIDE),
            vmem((events, 2 * cols - 1, 2, 8, 128), WIDE),
            dma((2,)),
            dma((9,)),
            dma((9,)),
            dma((10,)),
            dma((10,)),
            dma((cols,)),
            dma((cols,)),
            dma((groups,)),
            dma((groups,)),
            dma((groups,)),
            dma((groups,)),
            dma((apps,)),
            dma((apps,)),
            dma((ITERS, groups - 1)),
            dma((ITERS, groups - 1)),
            dma((events, groups - 1)),
            dma((events,)),
            dma((events, 2 * cols - 1)),
            dma((events,)),
            dma((2,)),
            dma((2,)),
        ],
        compiler_params=pltpu.CompilerParams(
            collective_id=0, has_side_effects=True, vmem_limit_bytes=60 << 20
        ),
        name="regmean_cg",
    )(acts, wts)


def solution(mesh):
    return jax.shard_map(
        local,
        mesh=mesh,
        in_specs=(P(None, "col", "row"), P(None, ("col", "row"), None)),
        out_specs=P("row", "col"),
        check_vma=False,
    )
```

```python
import jax
import jax.numpy as jnp
from jax import lax
from jax.experimental import pallas as pl
from jax.experimental.pallas import tpu as pltpu
from jax.sharding import PartitionSpec as P

ITERS = 3
BLEND_WEIGHT = 0.9
LOW = jnp.bfloat16
WIDE = jnp.float32
MESH = pl.DeviceIdType.MESH


def dot_nt(a, b):
    return lax.dot_general(a, b, (((1,), (1,)), ((), ())), preferred_element_type=WIDE)


def dot_nn(a, b):
    return lax.dot_general(a, b, (((1,), (0,)), ((), ())), preferred_element_type=WIDE)


def fold(v):
    rows, lanes = v.shape
    v = jnp.sum(v.reshape(rows // 8, 8, lanes), axis=0)
    out = v[:, 0:128]
    for i in range(1, lanes // 128):
        out = out + v[:, 128 * i : 128 * (i + 1)]
    return out


def kernel(
    acts, wts, out,
    xb, w1, wb, wt, dacc, dsum, v, own, psend, precv, pacc, asend, arecv, acc, r, d, x, ex, tile, sa, tile2, sb,
    lsem, xs_sem, xr_sem, fs_sem, fr_sem, w1_s, w1_r, w2_s, w2_r, w3_s, w3_r,
    rs_s, rs_r, ag_s, ag_r, s1_s, s1_r, s2_s, s2_r, ex_s, ex_r,
):
    groups, cols = 8, 8
    members, tok = acts.shape[0], acts.shape[1]
    width = acts.shape[2]
    part = v.shape[1]
    scale = BLEND_WEIGHT / (tok * cols)
    dscale = (1.0 - BLEND_WEIGHT) / (tok * cols)

    row = lax.axis_index("row")
    col = lax.axis_index("col")
    g = lax.div(row, 2)
    k = lax.rem(row, 2)
    x4 = lax.rem(g, 4)
    y2 = lax.div(g, 4)
    z = lax.div(col, 2)
    y = lax.rem(col, 2)
    q = col * 2 + k

    def copy(src, dst, ss, rs, to_row, to_col):
        return pltpu.make_async_remote_copy(
            src_ref=src, dst_ref=dst, send_sem=ss, recv_sem=rs,
            device_id=(to_row, to_col), device_id_type=MESH,
        )

    def peer(i):
        return (lax.rem(y2 + i // 4, 2)) * 4 + lax.rem(x4 + i, 4)

    def source(i):
        return (lax.rem(y2 + i // 4, 2)) * 4 + lax.rem(x4 + 4 - i % 4, 4)

    yp = 2 * y2 + y

    def plane(i):
        t = lax.rem(yp + i // 4, 4)
        return (lax.div(t, 2) * 4 + lax.rem(x4 + i, 4)) * 2 + k, z * 2 + lax.rem(t, 2)

    def pole(i):
        return 2 * g + lax.rem(k + i, 2), lax.rem(z + i // 2, 4) * 2 + y

    barrier = pltpu.get_barrier_semaphore()

    def greet(to_row, to_col):
        pl.semaphore_signal(barrier, inc=1, device_id=(to_row, to_col), device_id_type=MESH)

    @pl.loop(1, 2 * groups)
    def _(i):
        greet(*plane(i))

    @pl.loop(1, 2 * cols)
    def _(i):
        p = lax.rem(q + i, 2 * cols)
        greet(2 * g + lax.rem(p, 2), lax.div(p, 2))

    pl.semaphore_wait(barrier, 15 + 15)

    zp = lax.rem(z + 1, 4) * 2
    zm = lax.rem(z + 3, 4) * 2
    zf = lax.rem(z + 2, 4) * 2
    yo = 1 - y
    b_y, b_m, b_p = z * 2 + yo, zm + y, zp + y
    b_my, b_py, b_f, b_fy = zm + yo, zp + yo, zf + y, zf + yo
    c_y, c_p, c_m = z * 2 + yo, zp + y, zm + y
    half = members // 2
    lo, hi = pl.ds(0, half), pl.ds(half, half)
    other = 2 * g + 1 - k

    sends = []

    def start(c):
        c.start()
        sends.append(c)

    def forward(block, n, ms=None):
        ref = xb.at[k, block] if ms is None else xb.at[k, block, ms]
        start(copy(ref, ref, fs_sem.at[n], fr_sem.at[n], other, col))

    def w1_src(c):
        return wts.at[:, :, pl.ds(pl.multiple_of(c * 128, 128), 128)]

    def w1_copy(i):
        c = lax.rem(z + i // 2, 4) * 2 + lax.rem(y + i, 2)
        return copy(w1_src(c), w1.at[col], w1_s.at[i], w1_r.at[i], row, c)

    def w1_from(i):
        return lax.rem(z + 4 - i // 2, 4) * 2 + lax.rem(y + i, 2)

    local_w = pltpu.make_async_copy(w1_src(col), w1.at[col], lsem.at[1])
    local_w.start()

    @pl.loop(1, cols)
    def _(n):
        w1_copy(cols - n).start()

    local_x = pltpu.make_async_copy(acts, xb.at[k, col], lsem.at[0])
    local_x.start()
    mine = xb.at[k, col]
    start(copy(acts, mine, xs_sem.at[0], xr_sem.at[0], row, c_y))
    for n, to, ms in ((1, c_p, lo), (2, c_m, hi), (9, c_p, hi), (10, c_m, lo)):
        start(copy(acts.at[ms], xb.at[k, col, ms], xs_sem.at[n], xr_sem.at[n], row, to))
    start(copy(acts, mine, fs_sem.at[9], fr_sem.at[9], other, col))

    def diag(h, j, first=False):
        for m in range(members):
            t = xb[h, j, m].astype(WIDE)
            t = jnp.sum((t * t).reshape(tok // 8, 8, width), axis=0)
            if first:
                dacc[h, m] = t
            else:
                dacc[h, m] = dacc[h, m] + t

    local_x.wait()

    def fwait(n, block, ms=None):
        ref = xb.at[1 - k, block] if ms is None else xb.at[1 - k, block, ms]
        copy(ref, ref, fs_sem.at[n], fr_sem.at[n], other, col).wait_recv()

    def xwait(n, block, ms=None):
        ref = xb.at[k, block] if ms is None else xb.at[k, block, ms]
        copy(ref, ref, xs_sem.at[0], xr_sem.at[n], row, c_y).wait_recv()

    def relay(n, block, to, ms=None):
        ref = xb.at[k, block] if ms is None else xb.at[k, block, ms]
        start(copy(ref, ref, xs_sem.at[n], xr_sem.at[n], row, to))

    def w2_copy(i):
        p = peer(i)
        return copy(w1.at[p], wb.at[row], w2_s.at[i], w2_r.at[i], 2 * p + k, col)

    def w2_forward(i):
        ref = wb.at[2 * source(i) + k]
        return copy(ref, ref, w3_s.at[i], w3_r.at[i], other, col)

    local_w.wait()

    @pl.loop(1, cols)
    def _(n):
        i = cols - n
        ref = w1.at[w1_from(i)]
        copy(ref, ref, w1_s.at[i], w1_r.at[i], row, c_y).wait_recv()

    @pl.loop(1, groups)
    def _(n):
        w2_copy(groups - n).start()

    own_w = pltpu.make_async_copy(w1.at[g], wb.at[row], lsem.at[1])
    own_w.start()
    fwait(9, col)
    diag(0, col, True)
    diag(1, col, True)
    own_w.wait()
    w2_forward(0).start()
    xwait(1, b_m, lo)
    relay(5, b_m, c_p, lo)
    xwait(2, b_p, hi)
    relay(6, b_p, c_m, hi)
    xwait(0, b_y)
    relay(3, b_y, c_p)
    relay(4, b_y, c_m)
    forward(b_y, 0)
    xwait(9, b_m, hi)
    forward(b_m, 1)
    xwait(10, b_p, lo)
    forward(b_p, 2)

    @pl.loop(1, groups)
    def _(n):
        i = groups - n
        ref = wb.at[2 * source(i) + k]
        copy(ref, ref, w2_s.at[i], w2_r.at[i], row, c_y).wait_recv()
        w2_forward(i).start()

    @pl.loop(0, groups)
    def _(i):
        ref = wb.at[2 * source(i) + 1 - k]
        copy(ref, ref, w3_s.at[i], w3_r.at[i], other, col).wait_recv()

    for h in range(2):
        for m in range(members):
            w = wb[8 * h : 8 * h + 8, m].reshape(width, 2 * part)
            wt[m, h] = jnp.transpose(w.astype(WIDE)).astype(LOW)

    kpart = pl.ds(pl.multiple_of(k * part, part), part)

    def rs_copy(a, i):
        return copy(
            psend.at[a, i - 1], precv.at[a, i - 1], rs_s.at[a], rs_r.at[a],
            peer(i) * 2 + k, col,
        )

    def first_chunk(j):
        i = lax.rem(lax.div(j, 4) + y2, 2) * 4 + lax.rem(j + 4 - x4, 4)
        for m in range(members):
            t = dot_nt(wt[m, 0, kpart, :], xb[0, j, m]) + dot_nt(wt[m, 1, kpart, :], xb[1, j, m])
            own[:, m * tok : (m + 1) * tok] = t

        @pl.when(j == g)
        def _():
            pacc[...] = own[...]

        @pl.when(j != g)
        def _():
            psend[0, i - 1] = own[...].astype(LOW)
            rs_copy(0, i).start()

    def use(block):
        first_chunk(block)
        diag(0, block)
        diag(1, block)

    xwait(5, b_f, lo)
    relay(7, b_f, c_y, lo)
    forward(b_f, 5, lo)
    xwait(6, b_f, hi)
    relay(8, b_f, c_y, hi)
    forward(b_f, 6, hi)
    first_chunk(col)
    for n, b in ((0, b_y), (1, b_m), (2, b_p)):
        fwait(n, b)
        use(b)
    fwait(5, b_f, lo)
    fwait(6, b_f, hi)
    first_chunk(b_f)
    xwait(3, b_my)
    forward(b_my, 3)
    xwait(4, b_py)
    forward(b_py, 4)
    xwait(7, b_fy, lo)
    forward(b_fy, 7, lo)
    xwait(8, b_fy, hi)
    forward(b_fy, 8, hi)
    fwait(3, b_my)
    first_chunk(b_my)
    fwait(4, b_py)
    first_chunk(b_py)
    fwait(7, b_fy, lo)
    fwait(8, b_fy, hi)
    first_chunk(b_fy)
    for b in (b_f, b_my, b_py, b_fy):
        diag(0, b)
        diag(1, b)

    for h in range(2):
        rhs = None
        total = None
        for m in range(members):
            line = jnp.sum(dacc[h, m], axis=0, keepdims=True) * dscale
            term = line * wt[m, h, kpart, :].astype(WIDE)
            rhs = term if rhs is None else rhs + term
            total = line if total is None else total + line
        r[h] = rhs
        dsum[h] = jnp.broadcast_to(total, (8, width))

    def rs_wait(a):
        copy(precv.at[a], precv.at[a], rs_s.at[a], rs_r.at[a], row, c_y).wait_recv()

    def rs_total(a):
        s = precv[a, 0].astype(WIDE)
        for i in range(1, groups - 1):
            s = s + precv[a, i].astype(WIDE)
        return s

    def ag_copy(a, i):
        return copy(
            asend.at[a], arecv.at[a, i - 1], ag_s.at[a, i - 1], ag_r.at[a, i - 1],
            peer(i) * 2 + k, col,
        )

    def ag_start(a):
        @pl.loop(1, groups)
        def _(n):
            ag_copy(a, groups - n).start()

    def back_own(a):
        for h in range(2):
            acc[h] = dot_nn(asend[a], xb[h, g].reshape(members * tok, width))

    def back_rest(a):
        @pl.loop(1, groups)
        def _(n):
            i = groups - n
            j = source(i)
            ag_copy(a, i).wait_recv()
            p = arecv[a, i - 1]
            for h in range(2):
                acc[h] = acc[h] + dot_nn(p, xb[h, j].reshape(members * tok, width))

    def forth(a):
        def chunk(j):
            return dot_nt(v[0], xb[0, j].reshape(members * tok, width)) + dot_nt(
                v[1], xb[1, j].reshape(members * tok, width)
            )

        @pl.loop(1, groups)
        def _(n):
            i = groups - n
            psend[a, i - 1] = chunk(peer(i)).astype(LOW)
            rs_copy(a, i).start()

        own[...] = chunk(g)

    def s1_copy(e, i):
        return copy(tile.at[e], sa.at[e, i - 1], s1_s.at[e, i - 1], s1_r.at[e], *pole(i))

    def s1_start(e):
        @pl.loop(1, cols)
        def _(n):
            s1_copy(e, cols - n).start()

    def s2_copy(e, i):
        return copy(tile2.at[e], sb.at[e, i - 1], s2_s.at[e, i - 1], s2_r.at[e], *plane(i))

    def s1_finish(e):
        copy(sa.at[e], sa.at[e], s1_s.at[e, 0], s1_r.at[e], row, c_y).wait_recv()
        s = tile[e]
        for i in range(cols - 1):
            s = s + sa[e, i]
        tile2[e] = s

        @pl.loop(1, 2 * groups)
        def _(n):
            s2_copy(e, 2 * groups - n).start()

    def s2_finish(e):
        copy(sb.at[e], sb.at[e], s2_s.at[e, 0], s2_r.at[e], row, c_y).wait_recv()
        s = tile2[e]
        for i in range(2 * groups - 1):
            s = s + sb[e, i]
        return s

    rs_wait(0)
    asend[0] = (pacc[...] + rs_total(0)).astype(LOW)
    ag_start(0)
    back_own(0)
    back_rest(0)
    for h in range(2):
        r[h] = r[h] + scale * acc[h]
        d[h] = r[h]
        v[h] = r[h].astype(LOW)
        x[h] = jnp.zeros_like(r[h])

    rr = None
    for it in range(ITERS):
        a = it + 1
        forth(a)
        beta = None
        if it > 0:
            e = 2 * it - 1
            s1_finish(e)
            new = jnp.sum(s2_finish(e)[0])
            beta = new / rr
            rr = new
            for h in range(2):
                d[h] = r[h] + beta * d[h]
        if it == ITERS - 1:
            for n, ref in ((0, x), (1, d)):
                start(copy(ref.at[1 - k], ex.at[n], ex_s.at[n], ex_r.at[n], other, col))
        along = None
        norm = None
        for h in range(2):
            t = fold(d[h] * d[h] * dsum[h, 0:1])
            along = t if along is None else along + t
            if it == 0:
                t = fold(r[h] * r[h])
                norm = t if norm is None else norm + t
        rs_wait(a)
        p = own[...] + rs_total(a)
        if it > 0:
            p = p + beta * pacc[...]
        pacc[...] = p
        e = 2 * it
        tile[e, 0] = along + scale * fold(p * p)
        tile[e, 1] = along if norm is None else norm
        s1_start(e)
        if it < ITERS - 1:
            asend[a] = p.astype(LOW)
            ag_start(a)
            back_own(a)
        s1_finish(e)
        if it < ITERS - 1:
            back_rest(a)
        s = s2_finish(e)
        if it == 0:
            rr = jnp.sum(s[1])
        alpha = rr / jnp.sum(s[0])
        if it < ITERS - 1:
            norm = None
            for h in range(2):
                image = scale * acc[h] + dsum[h, 0:1] * d[h]
                x[h] = x[h] + alpha * d[h]
                rh = r[h] - alpha * image
                r[h] = rh
                v[h] = rh.astype(LOW)
                t = fold(rh * rh)
                norm = t if norm is None else norm + t
            e = 2 * it + 1
            tile[e, 0] = norm
            tile[e, 1] = norm
            s1_start(e)
        else:
            for n in range(2):
                copy(ex.at[n], ex.at[n], ex_s.at[n], ex_r.at[n], other, col).wait_recv()
            mine_part = x[k] + alpha * d[k]
            other_part = ex[0] + alpha * ex[1]

            @pl.when(k == 0)
            def _():
                out[...] = jnp.transpose(jnp.concatenate([mine_part, other_part], axis=0))

            @pl.when(k == 1)
            def _():
                out[...] = jnp.transpose(jnp.concatenate([other_part, mine_part], axis=0))

    for c in sends:
        c.wait_send()

    @pl.loop(1, cols)
    def _(i):
        w1_copy(i).wait_send()
        w2_copy(i).wait_send()

    @pl.loop(0, groups)
    def _(i):
        w2_forward(i).wait_send()

    for a in range(ITERS + 1):
        copy(psend.at[a], psend.at[a], rs_s.at[a], rs_r.at[a], row, c_y).wait_send()

    @pl.loop(1, groups)
    def _(i):
        for a in range(ITERS):
            ag_copy(a, i).wait_send()
        for e in range(2 * ITERS - 1):
            s1_copy(e, i).wait_send()

    @pl.loop(1, 2 * groups)
    def _(i):
        for e in range(2 * ITERS - 1):
            s2_copy(e, i).wait_send()


def local(acts, wts):
    members, tok, width = acts.shape
    cols = lax.axis_size("col")
    groups = lax.axis_size("row") // 2
    part = wts.shape[2] // (2 * cols)
    apps = ITERS + 1
    events = 2 * ITERS - 1
    chunk = members * tok
    vmem = pltpu.VMEM
    dma = pltpu.SemaphoreType.DMA
    return pl.pallas_call(
        kernel,
        out_shape=jax.ShapeDtypeStruct((width, 2 * part), WIDE),
        in_specs=[pl.BlockSpec(memory_space=pl.ANY)] * 2,
        out_specs=pl.BlockSpec(memory_space=pltpu.VMEM),
        scratch_shapes=[
            vmem((2, cols, members, tok, width), LOW),
            vmem((cols, members, wts.shape[1], 2 * part), LOW),
            vmem((2 * groups, members, wts.shape[1], 2 * part), LOW),
            vmem((members, 2, 2 * part, width), LOW),
            vmem((2, members, 8, width), WIDE),
            vmem((2, 8, width), WIDE),
            vmem((2, part, width), LOW),
            vmem((part, chunk), WIDE),
            vmem((apps, groups - 1, part, chunk), LOW),
            vmem((apps, groups - 1, part, chunk), LOW),
            vmem((part, chunk), WIDE),
            vmem((ITERS, part, chunk), LOW),
            vmem((ITERS, groups - 1, part, chunk), LOW),
            vmem((2, part, width), WIDE),
            vmem((2, part, width), WIDE),
            vmem((2, part, width), WIDE),
            vmem((2, part, width), WIDE),
            vmem((2, part, width), WIDE),
            vmem((events, 2, 8, 128), WIDE),
            vmem((events, cols - 1, 2, 8, 128), WIDE),
            vmem((events, 2, 8, 128), WIDE),
            vmem((events, 2 * groups - 1, 2, 8, 128), WIDE),
            dma((2,)),
            dma((11,)),
            dma((11,)),
            dma((10,)),
            dma((10,)),
            dma((cols,)),
            dma((cols,)),
            dma((groups,)),
            dma((groups,)),
            dma((groups,)),
            dma((groups,)),
            dma((apps,)),
            dma((apps,)),
            dma((ITERS, groups - 1)),
            dma((ITERS, groups - 1)),
            dma((events, cols - 1)),
            dma((events,)),
            dma((events, 2 * groups - 1)),
            dma((events,)),
            dma((2,)),
            dma((2,)),
        ],
        compiler_params=pltpu.CompilerParams(
            collective_id=0, has_side_effects=True, vmem_limit_bytes=60 << 20
        ),
        name="regmean_cg",
    )(acts, wts)


def solution(mesh):
    return jax.shard_map(
        local,
        mesh=mesh,
        in_specs=(P(None, "col", "row"), P(None, ("col", "row"), None)),
        out_specs=P("row", "col"),
        check_vma=False,
    )
```
